32 devices in a mesh: seq: 8 (over z, x), stream: 4 (over y, core).
Axes of the slice: x: 2, y: 2, z: 4, core: 2. Of those that a mesh axis runs over, the one named last changes fastest.
Arguments:
- tokens: bfloat16 [4, 4096, 768], P('stream', 'seq'), may hold values from -6 to 6
- segment_ids: int32 [4, 4096], P('stream', 'seq'), may hold values from -1 to 32, as said below
- query_key_value_weight: bfloat16 [768, 2304], replicated, may hold values from -0.21875 to 0.21875
- conv_kernel: bfloat16 [3, 2304], replicated, may hold values from -3 to 3
- attention_output_weight: bfloat16 [768, 768], replicated, may hold values from -0.875 to 0.875
- up_weight: bfloat16 [768, 3072], replicated, may hold values from -0.21875 to 0.21875
- down_weight: bfloat16 [3072, 768], replicated, may hold values from -0.109375 to 0.109375
- gain_attn: bfloat16 [768], replicated, may hold values from 0.5 to 1.5
- shift_attn: bfloat16 [768], replicated, may hold values from -3 to 3
- gain_ffn: bfloat16 [768], replicated, may hold values from 0.5 to 1.5
- shift_ffn: bfloat16 [768], replicated, may hold values from -3 to 3
- cotangent: bfloat16 [4, 4096, 768], P('stream', 'seq'), may hold values from -6 to 6
Outputs:
- out_tokens: bfloat16 [4, 4096, 768], P('stream', 'seq')
- grad_tokens: float32 [4, 4096, 768], P('stream', 'seq')
- grad_w_qkv: float32 [768, 2304], replicated
- grad_conv_kernel: float32 [3, 2304], replicated
- grad_w_out: float32 [768, 768], replicated
- grad_w_up: float32 [768, 3072], replicated
- grad_w_down: float32 [3072, 768], replicated
- grad_gain_attn: float32 [768], replicated
- grad_shift_attn: float32 [768], replicated
- grad_gain_ffn: float32 [768], replicated
- grad_shift_ffn: float32 [768], replicated
The draws below stay inside these ranges and needn't reach their ends.
Inputs may be any that keep to these rules, and one draw needn't show every extreme that they name: `segment_ids`: along each pack the document numbers never fall and differ between documents; each document fills 128 to 256 consecutive slots, one of 256 slots in every pack; the last document of every pack has the number 4096 // 128; slots between documents hold -1, and so does the last slot of each pack.
All inputs are finite; a program needn't handle non-finite values.
Results may differ from the reference program's by a relative error of at most 0.019.
Values may be sent and summed in bfloat16 or wider, within the bound.
No kernel may reach another device: no remote copies, remote signals or barrier semaphores. Data moves between devices by JAX's collectives and lax.ppermute only.
A program may use at most 256 MiB of HBM per device.

```python
import math
import jax
import jax.numpy as jnp
from jax import lax

D = 768
H = 12
HD = 64
FF = 3072
BLOCK = 512
MINLEN = 128
MAXLEN = 256
SLOTS = 4096
PACKS = 4


def draw_segment_ids(key, part):
    candidates = SLOTS // MINLEN + 1
    key_len, key_gap, key_kind = jax.random.split(key, 3)
    doc_lengths = jax.random.randint(key_len, (PACKS, candidates), MINLEN, MAXLEN + 1)
    doc_lengths = doc_lengths.at[:, 0].set(MAXLEN)
    kinds = jax.random.randint(key_kind, (PACKS, candidates), 0, 2)
    upper = jnp.where(kinds == 1, 3 * MINLEN // 2, MINLEN // 8)
    gaps = jax.random.randint(key_gap, (PACKS, candidates), 0, upper + 1)
    starts = jnp.cumsum(gaps + doc_lengths, axis=1) - doc_lengths
    ends = starts + doc_lengths
    kept = ends <= SLOTS - 1
    kept_count = jnp.sum(kept.astype(jnp.int32), axis=1)
    slot_pos = jnp.arange(SLOTS, dtype=jnp.int32)
    inside = (starts[:, None, :] <= slot_pos[None, :, None]) & (slot_pos[None, :, None] < ends[:, None, :]) & kept[:, None, :]
    numbers = jnp.arange(candidates, dtype=jnp.int32)
    found = jnp.sum(jnp.where(inside, numbers[None, None, :], 0), axis=2)
    found = jnp.where(found == kept_count[:, None] - 1, SLOTS // MINLEN, found)
    covered = jnp.any(inside, axis=2)
    return jnp.where(covered, found, -1).astype(jnp.int32)


def with_spikes(values, rng, source, target, parts, factor):
    def block_of(position):
        return (jnp.arange(values.shape[position]) // (values.shape[position] // parts)).reshape((-1,) + (1,) * (values.ndim - 1 - position))

    first = jax.random.permutation(rng, parts)[block_of(target)]
    far = (block_of(target) + parts // 2) % parts
    return jnp.where((block_of(source) == first) | (block_of(source) == far), factor * values, values)


def block_levels(stream_key, dims, shards, least, high):
    loudness, own = 1.0, jax.random.fold_in(stream_key, 6)
    for position, blocks in shards:
        steps = jnp.exp(jax.random.uniform(jax.random.fold_in(own, position), (blocks,), jnp.float32, least / len(shards), high / len(shards)))
        loudness = loudness * jnp.repeat(steps, dims[position] // blocks).reshape([-1 if axis == position else 1 for axis in range(len(dims))])
    return loudness


def centred(key, dims, scale, limit, cuts=(), kind=jnp.bfloat16):
    values = jax.random.normal(key, dims, jnp.float32) * scale
    if len(cuts) > 0:
        values = block_levels(key, dims, cuts, -0.22, 0.18) * values
    return jnp.clip(values, min=-limit, max=limit).astype(kind)


def noise_with(key, dims, scale, most, pieces, heavy, kind=jnp.bfloat16):
    values = scale * jax.random.normal(key, dims, jnp.float32)
    if pieces:
        values = values * block_levels(key, dims, pieces, -0.22, 0.18)
    return jnp.clip(with_spikes(values, jax.random.fold_in(key, 3), *heavy), -most, most).astype(kind)


def setup_inputs(seed: int = 0) -> dict:
    key_of = jax.random.split(jax.random.key(seed), 13)
    return {
        "tokens": centred(key_of[0], (PACKS, SLOTS, D), 1.0, 6.0, ((0, 4), (1, 8))),
        "segment_ids": draw_segment_ids(jax.random.fold_in(key_of[12], 71), 0),
        "query_key_value_weight": centred(key_of[2], (D, 3 * D), D ** -0.5, 0.21875),
        "conv_kernel": centred(key_of[3], (3, 3 * D), 0.6, 3.0),
        "attention_output_weight": centred(key_of[4], (D, D), (D // 16) ** -0.5, 0.875),
        "up_weight": centred(key_of[5], (D, FF), D ** -0.5, 0.21875),
        "down_weight": centred(key_of[6], (FF, D), FF ** -0.5, 0.109375),
        "gain_attn": jnp.clip(1.0 + 0.1 * jax.random.normal(key_of[7], (D,), jnp.float32), 0.5, 1.5).astype(jnp.bfloat16),
        "shift_attn": centred(key_of[8], (D,), 0.5, 3.0),
        "gain_ffn": jnp.clip(1.0 + 0.1 * jax.random.normal(key_of[9], (D,), jnp.float32), 0.5, 1.5).astype(jnp.bfloat16),
        "shift_ffn": centred(key_of[10], (D,), 0.5, 3.0),
        "cotangent": noise_with(key_of[11], (PACKS, SLOTS, D), 1.0, 6.0, ((0, 4), (1, 8)), (1, 2, 8, 2.0)),
    }


EPSILON = 1e-05
MASKED = -1e+30

@jax.custom_vjp
def low(v):
    return lax.optimization_barrier(v.astype(jnp.bfloat16)).astype(jnp.float32)

@jax.custom_vjp
def narrow_backward(v):
    return v

def low_keep(v):
    return (low(v), None)

def low_pass(kept, grad):
    return (grad,)

def back_keep(v):
    return (v, None)

def back_low(kept, grad):
    return (low(grad),)
low.defvjp(low_keep, low_pass)
narrow_backward.defvjp(back_keep, back_low)

def layer_norm(field, gain, shift):
    center = field - lax.optimization_barrier(jnp.mean(field, -1, keepdims=True))
    spread = lax.optimization_barrier(jnp.mean(center * center, -1, keepdims=True))
    return center * lax.rsqrt(spread + EPSILON) * gain + shift

def square_relu(field):
    return jnp.square(jnp.maximum(field, 0.0))

def causal_conv(field, segment_ids, kernel):
    result = kernel[0] * field
    for shift_by in (1, 2):
        moved = jnp.pad(field, ((0, 0), (shift_by, 0), (0, 0)))[:, :-shift_by]
        moved_ids = jnp.pad(segment_ids, ((0, 0), (shift_by, 0)), constant_values=-1)[:, :-shift_by]
        joined = ((moved_ids == segment_ids) & (segment_ids >= 0)).astype(jnp.float32)
        result = result + kernel[shift_by] * moved * joined[..., None]
    return result

def attend_block(queries, key_rows, value_rows, query_ids, key_ids, query_pos, key_pos):
    raw_scores = jnp.einsum('qhd,khd->hqk', queries, key_rows, precision=lax.Precision.HIGHEST)
    scores = narrow_backward(raw_scores) * (1.0 / math.sqrt(HD))
    allowed = (query_ids[:, None] == key_ids[None, :]) & (key_ids[None, :] >= 0)
    allowed = allowed & (key_pos[None, :] <= query_pos[:, None]) & (key_pos[None, :] >= 0)
    allowed = allowed | (key_pos[None, :] == query_pos[:, None])
    scores = jnp.where(allowed[None], scores, MASKED)
    probs = jax.nn.softmax(scores, axis=-1)
    return jnp.einsum('hqk,khd->qhd', low(probs), value_rows, precision=lax.Precision.HIGHEST)

def attention(queries, key_rows, value_rows, segment_ids):
    pack_count, slot_count = segment_ids.shape
    block_count = slot_count // BLOCK

    def split_rows(array_in):
        return array_in.reshape((pack_count, block_count, BLOCK) + array_in.shape[2:])

    def window(array_in, fill_value):
        own_rows = split_rows(array_in)
        prior_rows = jnp.concatenate([jnp.full_like(own_rows[:, :1], fill_value), own_rows[:, :-1]], 1)
        joined = jnp.concatenate([prior_rows, own_rows], 2)
        return joined.reshape((pack_count * block_count, 2 * BLOCK) + array_in.shape[2:])
    query_blocks = split_rows(queries).reshape((pack_count * block_count, BLOCK) + queries.shape[2:])
    query_ids = split_rows(segment_ids).reshape(pack_count * block_count, BLOCK)
    key_window = window(key_rows, 0.0)
    value_window = window(value_rows, 0.0)
    key_ids = window(segment_ids, -1)
    starts = jnp.tile(jnp.arange(block_count, dtype=jnp.int32) * BLOCK, pack_count)

    def one_block(inputs):
        block_q, block_k, block_v, ids_q, ids_k, start_slot = inputs
        query_pos = start_slot + jnp.arange(BLOCK, dtype=jnp.int32)
        key_pos = start_slot - BLOCK + jnp.arange(2 * BLOCK, dtype=jnp.int32)
        return attend_block(block_q, block_k, block_v, ids_q, ids_k, query_pos, key_pos)
    outputs = lax.map(jax.checkpoint(one_block), (query_blocks, key_window, value_window, query_ids, key_ids, starts))
    return outputs.reshape(queries.shape)

def reference(tokens, segment_ids, query_key_value_weight, conv_kernel, attention_output_weight, up_weight, down_weight, gain_attn, shift_attn, gain_ffn, shift_ffn, cotangent):
    active_token_mask = (segment_ids >= 0).astype(jnp.float32)[..., None]
    highest_precision = lax.Precision.HIGHEST

    def forward(inputs, query_key_value_matrix, kernel, output_weight_matrix, up_weight_matrix, down_weight_matrix, gain_one, shift_one, gain_two, shift_two):
        normalized_first = low(layer_norm(inputs, gain_one, shift_one))
        mixed_query_key_value = narrow_backward(jnp.einsum('jmc,ct->jmt', normalized_first, query_key_value_matrix, precision=highest_precision))
        convolved = low(causal_conv(mixed_query_key_value, segment_ids, kernel))
        head_shape = inputs.shape[:2] + (H, HD)
        queries = convolved[..., :D].reshape(head_shape)
        key_rows = convolved[..., D:2 * D].reshape(head_shape)
        value_rows = convolved[..., 2 * D:].reshape(head_shape)
        attention_result = attention(queries, key_rows, value_rows, segment_ids).reshape(inputs.shape)
        attention_result = low(narrow_backward(attention_result))
        residual_branch = narrow_backward(jnp.einsum('jmc,ct->jmt', attention_result, output_weight_matrix, precision=highest_precision))
        middle_state = inputs + active_token_mask * residual_branch
        normalized_second = low(layer_norm(middle_state, gain_two, shift_two))
        hidden_state = narrow_backward(jnp.einsum('zha,ay->zhy', normalized_second, up_weight_matrix, precision=highest_precision))
        activated_hidden = low(square_relu(hidden_state))
        return middle_state + active_token_mask * jnp.einsum('nxg,gi->nxi', activated_hidden, down_weight_matrix, precision=highest_precision)
    primals = tuple((array_in.astype(jnp.float32) for array_in in (tokens, query_key_value_weight, conv_kernel, attention_output_weight, up_weight, down_weight, gain_attn, shift_attn, gain_ffn, shift_ffn)))
    result, pullback = jax.vjp(forward, *primals)
    grads = pullback(cotangent.astype(jnp.float32))
    return (result.astype(jnp.bfloat16), grads[0], grads[1], grads[2], grads[3], grads[4], grads[5], grads[6], grads[7], grads[8], grads[9])
```

```python
import math

import jax
import jax.numpy as jnp
from jax import lax
from jax.sharding import PartitionSpec as P

H = 12
HD = 64


EPSILON = 1e-05
MASKED = -1e30


def passed_along(block, axis, distance):
    devices = range(lax.axis_size(axis))
    route = [(i - distance, i) for i in devices if i - distance in devices]
    return lax.ppermute(block, axis, route)


def layer_norm(field, gain, shift):
    center = field - jnp.mean(field, -1, keepdims=True)
    spread = jnp.mean(center * center, -1, keepdims=True)
    return center * lax.rsqrt(spread + EPSILON) * gain + shift


def square_relu(field):
    return jnp.square(jnp.maximum(field, 0.0))


def conv_local(extended, kernel, same_one, same_two):
    row_count = extended.shape[1] - 2
    result = kernel[0] * extended[:, 2:]
    result = result + kernel[1] * extended[:, 1 : row_count + 1] * same_one
    result = result + kernel[2] * extended[:, :row_count] * same_two
    return result


def pair_scores(queries, key_rows, query_ids, key_ids, query_pos, key_pos):
    raw_scores = jnp.einsum(
        "sqhd,skhd->shqk", queries, key_rows, preferred_element_type=jnp.float32
    )
    allowed = (query_ids[:, :, None] == key_ids[:, None, :]) & (key_ids[:, None, :] >= 0)
    allowed = (
        allowed
        & (key_pos[None, None, :] <= query_pos[None, :, None])
        & (key_pos[None, None, :] >= 0)
    )
    allowed = allowed | (key_pos[None, None, :] == query_pos[None, :, None])
    return jnp.where(allowed[:, None], raw_scores * (1.0 / math.sqrt(HD)), MASKED)


def on_device(
    tokens,
    segment_ids,
    query_key_value_weight,
    conv_kernel,
    attention_output_weight,
    up_weight,
    down_weight,
    gain_attn,
    shift_attn,
    gain_ffn,
    shift_ffn,
    cotangent,
):
    pack_count, slot_count, model_width = tokens.shape
    device_at = lax.axis_index("seq")
    slot_steps = jnp.arange(slot_count, dtype=jnp.int32)
    query_pos = device_at * slot_count + slot_steps
    own_live = segment_ids >= 0
    active_token_mask = own_live.astype(jnp.float32)[..., None]
    inputs = tokens.astype(jnp.float32)
    normalized_first, norm_one_back = jax.vjp(
        layer_norm, inputs, gain_attn.astype(jnp.float32), shift_attn.astype(jnp.float32)
    )
    normalized_first_narrow = normalized_first.astype(jnp.bfloat16)
    mixed_query_key_value = jnp.einsum(
        "jmc,ct->jmt",
        normalized_first_narrow,
        query_key_value_weight,
        preferred_element_type=jnp.float32,
    )
    halo_rows, halo_ids = passed_along(
        (mixed_query_key_value[:, -2:], segment_ids[:, -2:]), "seq", 1
    )
    extended = jnp.concatenate([halo_rows, mixed_query_key_value], 1)
    extended_ids = jnp.concatenate([halo_ids, segment_ids], 1)
    same_one = ((extended_ids[:, 1 : slot_count + 1] == segment_ids) & own_live).astype(
        jnp.float32
    )[..., None]
    same_two = ((extended_ids[:, :slot_count] == segment_ids) & own_live).astype(jnp.float32)[
        ..., None
    ]
    convolved, conv_back = jax.vjp(
        lambda field, weights: conv_local(field, weights, same_one, same_two),
        extended,
        conv_kernel.astype(jnp.float32),
    )
    conv_low = convolved.astype(jnp.bfloat16)
    head_shape = (pack_count, slot_count, H, HD)
    queries = conv_low[..., :model_width].reshape(head_shape)
    pair_kv = conv_low[..., model_width:]
    prior_kv, prior_ids = passed_along((pair_kv, segment_ids), "seq", 1)
    shard_kv = jnp.stack([prior_kv, pair_kv])
    shard_ids = jnp.stack([prior_ids, segment_ids])
    shard_at = device_at - 1 + jnp.arange(2, dtype=jnp.int32)
    shard_total = shard_kv.shape[0]
    first_id = jnp.min(jnp.where(own_live, segment_ids, 1 << 30))

    def shard_view(shard):
        block_kv = lax.dynamic_index_in_dim(shard_kv, shard, 0, keepdims=False)
        key_rows = block_kv[..., :model_width].reshape(head_shape)
        value_rows = block_kv[..., model_width:].reshape(head_shape)
        key_ids = lax.dynamic_index_in_dim(shard_ids, shard, 0, keepdims=False)
        owner = lax.dynamic_index_in_dim(shard_at, shard, 0, keepdims=False)
        key_pos = owner * slot_count + slot_steps
        useful = (owner == device_at) | (owner < device_at) & (owner >= 0) & (
            jnp.max(key_ids) >= first_id
        )
        return (key_rows, value_rows, key_ids, key_pos, useful)

    def keep_state(state):
        return state

    def top_step(shard, state):
        key_rows, value_rows, key_ids, key_pos, useful = shard_view(shard)

        def top_work(inner):
            row_top, row_total = inner
            scores = pair_scores(queries, key_rows, segment_ids, key_ids, query_pos, key_pos)
            new_top = jnp.maximum(row_top, jnp.max(scores, -1))
            row_total = row_total * jnp.exp(row_top - new_top) + jnp.sum(
                jnp.exp(scores - new_top[..., None]), -1
            )
            return (new_top, row_total)

        return lax.cond(useful, top_work, keep_state, state)

    stat_shape = (pack_count, H, slot_count)
    row_top, row_total = lax.fori_loop(
        0,
        shard_total,
        top_step,
        (jnp.full(stat_shape, MASKED, jnp.float32), jnp.zeros(stat_shape, jnp.float32)),
    )
    log_total = row_top + jnp.log(row_total)

    def probs_for(key_rows, key_ids, key_pos):
        scores = pair_scores(queries, key_rows, segment_ids, key_ids, query_pos, key_pos)
        return jnp.exp(scores - log_total[..., None])

    def out_step(shard, state):
        key_rows, value_rows, key_ids, key_pos, useful = shard_view(shard)

        def out_work(inner):
            probs = probs_for(key_rows, key_ids, key_pos)
            return inner + jnp.einsum(
                "shqk,skhd->sqhd",
                probs.astype(jnp.bfloat16),
                value_rows,
                preferred_element_type=jnp.float32,
            )

        return lax.cond(useful, out_work, keep_state, state)

    attention_result = lax.fori_loop(0, shard_total, out_step, jnp.zeros(head_shape, jnp.float32))
    attention_result = attention_result.reshape(pack_count, slot_count, model_width).astype(
        jnp.bfloat16
    )
    residual_branch = jnp.einsum(
        "jmc,ct->jmt", attention_result, attention_output_weight, preferred_element_type=jnp.float32
    )
    middle_state = inputs + active_token_mask * residual_branch
    normalized_second, norm_two_back = jax.vjp(
        layer_norm, middle_state, gain_ffn.astype(jnp.float32), shift_ffn.astype(jnp.float32)
    )
    normalized_second_narrow = normalized_second.astype(jnp.bfloat16)
    hidden_state = jnp.einsum(
        "zha,ay->zhy", normalized_second_narrow, up_weight, preferred_element_type=jnp.float32
    )
    activated_hidden, relu_back = jax.vjp(square_relu, hidden_state)
    activated_narrow = activated_hidden.astype(jnp.bfloat16)
    feedforward_output = jnp.einsum(
        "nxg,gi->nxi", activated_narrow, down_weight, preferred_element_type=jnp.float32
    )
    out_tokens = (middle_state + active_token_mask * feedforward_output).astype(jnp.bfloat16)
    grad_out = cotangent.astype(jnp.float32)
    gradient_residual_branch = (active_token_mask * grad_out).astype(jnp.bfloat16)
    grad_w_down = jnp.einsum(
        "ipr,iph->rh",
        activated_narrow,
        gradient_residual_branch,
        preferred_element_type=jnp.float32,
    )
    gradient_activated = jnp.einsum(
        "owr,ar->owa", gradient_residual_branch, down_weight, preferred_element_type=jnp.float32
    )
    gradient_hidden_state = relu_back(gradient_activated)[0].astype(jnp.bfloat16)
    grad_w_up = jnp.einsum(
        "jtw,jth->wh",
        normalized_second_narrow,
        gradient_hidden_state,
        preferred_element_type=jnp.float32,
    )
    grad_normed_two = jnp.einsum(
        "ytw,pw->ytp", gradient_hidden_state, up_weight, preferred_element_type=jnp.float32
    )
    grad_middle_part, grad_gain_ffn, grad_shift_ffn = norm_two_back(grad_normed_two)
    grad_middle = grad_out + grad_middle_part
    gradient_attention_branch = (active_token_mask * grad_middle).astype(jnp.bfloat16)
    grad_w_out = jnp.einsum(
        "tir,tiv->rv",
        attention_result,
        gradient_attention_branch,
        preferred_element_type=jnp.float32,
    )
    grad_heads = (
        jnp.einsum(
            "tig,ag->tia",
            gradient_attention_branch,
            attention_output_weight,
            preferred_element_type=jnp.float32,
        )
        .astype(jnp.bfloat16)
        .reshape(head_shape)
    )

    def delta_step(shard, state):
        key_rows, value_rows, key_ids, key_pos, useful = shard_view(shard)

        def delta_work(inner):
            probs = probs_for(key_rows, key_ids, key_pos)
            grad_probs = jnp.einsum(
                "sqhd,skhd->shqk", grad_heads, value_rows, preferred_element_type=jnp.float32
            )
            return inner + jnp.sum(probs * grad_probs, -1)

        return lax.cond(useful, delta_work, keep_state, state)

    row_delta = lax.fori_loop(0, shard_total, delta_step, jnp.zeros(stat_shape, jnp.float32))

    def grad_step(shard, state):
        key_rows, value_rows, key_ids, key_pos, useful = shard_view(shard)

        def grad_work(inner):
            grad_queries, key_terms = inner
            probs = probs_for(key_rows, key_ids, key_pos)
            grad_probs = jnp.einsum(
                "sqhd,skhd->shqk", grad_heads, value_rows, preferred_element_type=jnp.float32
            )
            grad_scores = (
                probs * (grad_probs - row_delta[..., None]) * (1.0 / math.sqrt(HD))
            ).astype(jnp.bfloat16)
            grad_queries = grad_queries + jnp.einsum(
                "shqk,skhd->sqhd", grad_scores, key_rows, preferred_element_type=jnp.float32
            )
            grad_keys = jnp.einsum(
                "shqk,sqhd->skhd", grad_scores, queries, preferred_element_type=jnp.float32
            )
            grad_values = jnp.einsum(
                "shqk,sqhd->skhd",
                probs.astype(jnp.bfloat16),
                grad_heads,
                preferred_element_type=jnp.float32,
            )
            key_piece = jnp.concatenate(
                [
                    grad_keys.reshape(pack_count, slot_count, model_width),
                    grad_values.reshape(pack_count, slot_count, model_width),
                ],
                -1,
            )
            key_terms = lax.dynamic_update_index_in_dim(key_terms, key_piece, shard, 0)
            return (grad_queries, key_terms)

        return lax.cond(useful, grad_work, keep_state, state)

    term_init = jnp.zeros((shard_total, pack_count, slot_count, 2 * model_width), jnp.float32)
    grad_queries, key_terms = lax.fori_loop(
        0, shard_total, grad_step, (jnp.zeros(head_shape, jnp.float32), term_init)
    )
    grad_kv = key_terms[1] + passed_along(key_terms[0].astype(jnp.bfloat16), "seq", -1).astype(
        jnp.float32
    )
    grad_conv = jnp.concatenate(
        [grad_queries.reshape(pack_count, slot_count, model_width), grad_kv], -1
    )
    grad_extended, grad_kernel = conv_back(grad_conv)
    back_rows = passed_along(grad_extended[:, :2], "seq", -1)
    gradient_mixed_projection = grad_extended[:, 2:]
    gradient_mixed_projection = jnp.concatenate(
        [gradient_mixed_projection[:, :-2], gradient_mixed_projection[:, -2:] + back_rows], 1
    ).astype(jnp.bfloat16)
    grad_w_qkv = jnp.einsum(
        "tir,tiv->rv",
        normalized_first_narrow,
        gradient_mixed_projection,
        preferred_element_type=jnp.float32,
    )
    gradient_normalized_first = jnp.einsum(
        "tig,ag->tia",
        gradient_mixed_projection,
        query_key_value_weight,
        preferred_element_type=jnp.float32,
    )
    grad_input_part, grad_gain_attn, grad_shift_attn = norm_one_back(gradient_normalized_first)
    grad_tokens = grad_middle + grad_input_part
    grads = [
        grad_w_qkv,
        grad_kernel,
        grad_w_out,
        grad_w_up,
        grad_w_down,
        grad_gain_attn,
        grad_shift_attn,
        grad_gain_ffn,
        grad_shift_ffn,
    ]
    both = ("seq", "stream")
    small = [grads[1].reshape(-1)] + grads[5:]
    small_sum = lax.psum(jnp.concatenate(small), both)
    big = {
        at: lax.psum(grads[at].astype(jnp.bfloat16), both).astype(jnp.float32)
        for at in (4, 3, 2, 0)
    }
    results = []
    offset = 0
    for at, piece in enumerate(grads):
        if at in big:
            results.append(big[at])
        else:
            results.append(small_sum[offset : offset + piece.size].reshape(piece.shape))
            offset = offset + piece.size
    return (
        out_tokens,
        grad_tokens,
        results[0],
        results[1],
        results[2],
        results[3],
        results[4],
        results[5],
        results[6],
        results[7],
        results[8],
    )


def solution(mesh):
    return jax.shard_map(
        on_device,
        mesh=mesh,
        in_specs=(
            P("stream", "seq", None),
            P("stream", "seq"),
            P(),
            P(),
            P(),
            P(),
            P(),
            P(),
            P(),
            P(),
            P(),
            P("stream", "seq", None),
        ),
        out_specs=(
            P("stream", "seq", None),
            P("stream", "seq", None),
            P(),
            P(),
            P(),
            P(),
            P(),
            P(),
            P(),
            P(),
            P(),
        ),
        check_vma=False,
    )
```

```python
import jax
import jax.numpy as jnp
from jax import lax
from jax.experimental import pallas as pl
from jax.experimental.pallas import tpu as pltpu
from jax.sharding import PartitionSpec as P

HD = 64
PAIR = 2 * HD
EPSILON = 1e-05
MASKED = -1e30
REACH = 256
TILE = 128
WINDOW = REACH + TILE


def layer_norm(field, gain, shift):
    center = field - jnp.mean(field, -1, keepdims=True)
    spread = jnp.mean(center * center, -1, keepdims=True)
    return center * lax.rsqrt(spread + EPSILON) * gain + shift


def dot(left, right, left_dim, right_dim):
    return lax.dot_general(
        left, right, (((left_dim,), (right_dim,)), ((), ())), preferred_element_type=jnp.float32
    )


def both_heads(rows):
    first = lax.broadcasted_iota(jnp.int32, rows.shape, 1) < HD
    zero = jnp.zeros_like(rows)
    return jnp.concatenate([jnp.where(first, rows, zero), jnp.where(first, zero, rows)], 0)


def own_lanes(rows):
    half = rows.shape[0] // 2
    first = lax.broadcasted_iota(jnp.int32, (half, rows.shape[1]), 1) < HD
    return jnp.where(first, rows[:half], rows[half:])


def attend_kernel(
    uq, uk, uv, kq, kk, kv, same_one, same_two, key_ids, query_ids, out, probs, cq, ck, cv, bias
):
    tiles = query_ids.shape[1] // TILE

    @pl.when(pl.program_id(0) == 0)
    def _():
        for t in range(tiles):
            rows = lax.broadcasted_iota(jnp.int32, (WINDOW, TILE), 0)
            columns = lax.broadcasted_iota(jnp.int32, (WINDOW, TILE), 1) + REACH
            equal = key_ids[t * TILE : t * TILE + WINDOW] == query_ids[:, t * TILE : (t + 1) * TILE]
            allowed = (equal & (rows <= columns)) | (rows == columns)
            tile_bias = jnp.where(allowed, 0.0, MASKED)
            bias[t] = jnp.concatenate([tile_bias, tile_bias], 1)

    one, two = same_one[...], same_two[...]

    def convolved(u, taps):
        field = u[...].astype(jnp.float32)
        return (
            taps[0:1] * field
            + taps[1:2] * pltpu.roll(field, 1, 0) * one
            + taps[2:3] * pltpu.roll(field, 2, 0) * two
        )

    cq[...] = convolved(uq, kq)[REACH:].astype(jnp.bfloat16) * 0.125
    ck[...] = convolved(uk, kk).astype(jnp.bfloat16)
    cv[...] = convolved(uv, kv).astype(jnp.bfloat16)
    for t in range(tiles):
        window = slice(t * TILE, t * TILE + WINDOW)
        own = slice(t * TILE, (t + 1) * TILE)
        scores = dot(ck[window], both_heads(cq[own]), 1, 1) + bias[t]
        powers = jnp.exp(scores - jnp.max(scores, 0, keepdims=True))
        narrow = (powers * (1.0 / jnp.sum(powers, 0, keepdims=True))).astype(jnp.bfloat16)
        probs[0, t] = narrow
        out[own] = own_lanes(dot(narrow, cv[window], 0, 0)).astype(jnp.bfloat16)


def attend_back_kernel(
    grad_out, probs, cq, ck, cv, uq, uk, uv, kq, kk, kv, same_one, same_two,
    gu, gtaps, gq_rows, gk_rows, gv_rows,
):
    head = pl.program_id(0)
    width = gu.shape[1] // 3
    tiles = grad_out.shape[0] // TILE
    gq_rows[:REACH] = jnp.zeros((REACH, PAIR), jnp.float32)
    gk_rows[...] = jnp.zeros_like(gk_rows)
    gv_rows[...] = jnp.zeros_like(gv_rows)
    for t in range(tiles):
        window = slice(t * TILE, t * TILE + WINDOW)
        own = slice(t * TILE, (t + 1) * TILE)
        grads = both_heads(grad_out[own])
        narrow = probs[0, t]
        wide = narrow.astype(jnp.float32)
        grad_probs = dot(cv[window], grads, 1, 1)
        delta = jnp.sum(wide * grad_probs, 0, keepdims=True)
        grad_scores = (wide * (grad_probs - delta)).astype(jnp.bfloat16)
        gk_rows[window] += dot(grad_scores, both_heads(cq[own]), 1, 0)
        gv_rows[window] += dot(narrow, grads, 1, 0)
        gq_rows[REACH + t * TILE : REACH + (t + 1) * TILE] = (
            own_lanes(dot(grad_scores, ck[window], 0, 0)) * 0.125
        )
    one, two = same_one[...], same_two[...]
    last = gq_rows.shape[0]
    for part, (rows, u, taps) in enumerate(
        ((gq_rows, uq, kq), (gk_rows, uk, kk), (gv_rows, uv, kv))
    ):
        field = u[...].astype(jnp.float32)
        grad = rows[...]
        grad_one, grad_two = grad * one, grad * two
        place = pl.ds(pl.multiple_of(part * width + head * PAIR, PAIR), PAIR)
        gu[:, place] = (
            taps[0:1] * grad
            + taps[1:2] * pltpu.roll(grad_one, last - 1, 0)
            + taps[2:3] * pltpu.roll(grad_two, last - 2, 0)
        ).astype(jnp.bfloat16)
        gtaps[0:1, place] = jnp.sum(grad * field, 0, keepdims=True)
        gtaps[1:2, place] = jnp.sum(grad_one * pltpu.roll(field, 1, 0), 0, keepdims=True)
        gtaps[2:3, place] = jnp.sum(grad_two * pltpu.roll(field, 2, 0), 0, keepdims=True)


def column_specs(rows, pairs):
    return [
        pl.BlockSpec((rows, PAIR), lambda h, part=part: (0, part * pairs + h)) for part in range(3)
    ]


def whole(shape):
    return pl.BlockSpec(shape, lambda h: (0,) * len(shape))


def attend(mixed, taps, same_one, same_two, key_ids, query_ids):
    rows, width = mixed.shape[0], mixed.shape[1] // 3
    slots, pairs = rows - REACH, width // PAIR
    tiles = slots // TILE
    block = lambda count: pl.BlockSpec((count, PAIR), lambda h: (0, h))
    return pl.pallas_call(
        attend_kernel,
        grid=(pairs,),
        in_specs=column_specs(rows, pairs)
        + column_specs(3, pairs)
        + [whole((rows, 1))] * 3
        + [whole((1, slots))],
        out_specs=[
            block(slots),
            pl.BlockSpec((1, tiles, WINDOW, 2 * TILE), lambda h: (h, 0, 0, 0)),
            block(slots),
            block(rows),
            block(rows),
        ],
        out_shape=[
            jax.ShapeDtypeStruct((slots, width), jnp.bfloat16),
            jax.ShapeDtypeStruct((pairs, tiles, WINDOW, 2 * TILE), jnp.bfloat16),
            jax.ShapeDtypeStruct((slots, width), jnp.bfloat16),
            jax.ShapeDtypeStruct((rows, width), jnp.bfloat16),
            jax.ShapeDtypeStruct((rows, width), jnp.bfloat16),
        ],
        scratch_shapes=[pltpu.VMEM((tiles, WINDOW, 2 * TILE), jnp.float32)],
        name="attend",
    )(mixed, mixed, mixed, taps, taps, taps, same_one, same_two, key_ids, query_ids)


def attend_back(grad_heads, kept, mixed, taps, same_one, same_two):
    rows, width = mixed.shape[0], mixed.shape[1] // 3
    slots, pairs = rows - REACH, width // PAIR
    tiles = slots // TILE
    probs, cq, ck, cv = kept
    block = lambda count: pl.BlockSpec((count, PAIR), lambda h: (0, h))
    return pl.pallas_call(
        attend_back_kernel,
        grid=(pairs,),
        in_specs=[
            block(slots),
            pl.BlockSpec((1, tiles, WINDOW, 2 * TILE), lambda h: (h, 0, 0, 0)),
            block(slots),
            block(rows),
            block(rows),
        ]
        + column_specs(rows, pairs)
        + column_specs(3, pairs)
        + [whole((rows, 1))] * 2,
        out_specs=[whole((rows, 3 * width)), whole((3, 3 * width))],
        out_shape=[
            jax.ShapeDtypeStruct((rows, 3 * width), jnp.bfloat16),
            jax.ShapeDtypeStruct((3, 3 * width), jnp.float32),
        ],
        scratch_shapes=[pltpu.VMEM((rows, PAIR), jnp.float32)] * 3,
        name="attend_back",
    )(grad_heads, probs, cq, ck, cv, mixed, mixed, mixed, taps, taps, taps, same_one, same_two)


def passed_along(block, axis, distance):
    devices = range(lax.axis_size(axis))
    route = [(i - distance, i) for i in devices if i - distance in devices]
    return lax.ppermute(block, axis, route)


def summed(grads, small):
    both = ("seq", "stream")
    small_sum = lax.psum(jnp.concatenate([piece.reshape(-1) for piece in small]), both)
    big = [lax.psum(piece, both).astype(jnp.float32) for piece in grads]
    parts, offset = [], 0
    for piece in small:
        parts.append(small_sum[offset : offset + piece.size].reshape(piece.shape))
        offset += piece.size
    return big, parts


def product(left, right, left_dim, right_dim, dtype=jnp.float32):
    return dot(left, right, left_dim, right_dim).astype(dtype)


def on_device(
    tokens,
    segment_ids,
    query_key_value_weight,
    conv_kernel,
    attention_output_weight,
    up_weight,
    down_weight,
    gain_attn,
    shift_attn,
    gain_ffn,
    shift_ffn,
    cotangent,
):
    narrow = jnp.bfloat16
    own_tokens, ids, grad_low = tokens[0], segment_ids[0], cotangent[0]
    prior_tokens, prior_ids = passed_along((own_tokens[-REACH:], ids[-REACH:]), "seq", 1)
    prior_ids = jnp.where(lax.axis_index("seq") > 0, prior_ids, -1)
    rows_ids = jnp.concatenate([prior_ids, ids])
    live_rows = rows_ids >= 0

    def same(distance):
        moved = jnp.concatenate([jnp.full((distance,), -1, jnp.int32), rows_ids[:-distance]])
        return ((moved == rows_ids) & live_rows).astype(jnp.float32)[:, None]

    same_one, same_two = same(1), same(2)
    key_ids = jnp.where(live_rows, rows_ids, -2)[:, None]
    live = (ids >= 0).astype(jnp.float32)[:, None]
    taps = conv_kernel.astype(jnp.float32)

    rows = jnp.concatenate([prior_tokens, own_tokens]).astype(jnp.float32)
    first, first_back = jax.vjp(
        layer_norm, rows, gain_attn.astype(jnp.float32), shift_attn.astype(jnp.float32)
    )
    first = first.astype(narrow)
    mixed = product(first, query_key_value_weight, 1, 0, narrow)
    attended, *kept = attend(mixed, taps, same_one, same_two, key_ids, ids[None])

    middle = own_tokens.astype(jnp.float32) + live * product(attended, attention_output_weight, 1, 0)
    second, second_back = jax.vjp(
        layer_norm, middle, gain_ffn.astype(jnp.float32), shift_ffn.astype(jnp.float32)
    )
    second = second.astype(narrow)
    hidden = jnp.maximum(product(second, up_weight, 1, 0), 0.0)
    active = jnp.square(hidden).astype(narrow)
    grad = grad_low.astype(jnp.float32)
    grad_branch = (live * grad).astype(narrow)
    grad_w_down = product(active, grad_branch, 0, 0, narrow)
    grad_hidden = (product(grad_branch, down_weight, 1, 1) * (2.0 * hidden)).astype(narrow)
    grad_w_up = product(second, grad_hidden, 0, 0, narrow)
    out_tokens = (middle + live * product(active, down_weight, 1, 0)).astype(narrow)
    grad_part, grad_gain_ffn, grad_shift_ffn = second_back(product(grad_hidden, up_weight, 1, 1))
    grad_middle = grad + grad_part
    grad_attended = (live * grad_middle).astype(narrow)
    grad_w_out = product(attended, grad_attended, 0, 0, narrow)
    grad_heads = product(grad_attended, attention_output_weight, 1, 1, narrow)

    grad_mixed, grad_taps = attend_back(grad_heads, kept, mixed, taps, same_one, same_two)
    grad_w_qkv = product(first, grad_mixed, 0, 0, narrow)
    grad_rows, grad_gain_attn, grad_shift_attn = first_back(
        product(grad_mixed, query_key_value_weight, 1, 1)
    )
    later = passed_along(grad_rows[:REACH].astype(narrow), "seq", -1)
    grad_tokens = grad_middle + grad_rows[REACH:]
    slots = grad_tokens.shape[0]
    grad_tokens = grad_tokens + jnp.pad(
        later.astype(jnp.float32), ((slots - REACH, 0), (0, 0))
    )
    big, parts = summed(
        [grad_w_down, grad_w_up, grad_w_out, grad_w_qkv],
        [grad_taps, grad_gain_attn, grad_shift_attn, grad_gain_ffn, grad_shift_ffn],
    )
    return (
        out_tokens[None],
        grad_tokens[None],
        big[3],
        parts[0],
        big[2],
        big[1],
        big[0],
        parts[1],
        parts[2],
        parts[3],
        parts[4],
    )


def solution(mesh):
    return jax.shard_map(
        on_device,
        mesh=mesh,
        in_specs=(
            P("stream", "seq", None),
            P("stream", "seq"),
            P(),
            P(),
            P(),
            P(),
            P(),
            P(),
            P(),
            P(),
            P(),
            P("stream", "seq", None),
        ),
        out_specs=(
            P("stream", "seq", None),
            P("stream", "seq", None),
            P(),
            P(),
            P(),
            P(),
            P(),
            P(),
            P(),
            P(),
            P(),
        ),
        check_vma=False,
    )
```

```python
import jax
import jax.numpy as jnp
from jax import lax
from jax.experimental import pallas as pl
from jax.experimental.pallas import tpu as pltpu
from jax.sharding import PartitionSpec as P

HD = 64
PAIR = 2 * HD
EPSILON = 1e-05
MASKED = -1e30
REACH = 256
TILE = 128
WINDOW = REACH + TILE


def layer_norm(field, gain, shift):
    center = field - jnp.mean(field, -1, keepdims=True)
    spread = jnp.mean(center * center, -1, keepdims=True)
    return center * lax.rsqrt(spread + EPSILON) * gain + shift


def dot(left, right, left_dim, right_dim):
    return lax.dot_general(
        left, right, (((left_dim,), (right_dim,)), ((), ())), preferred_element_type=jnp.float32
    )


def both_heads(rows):
    first = lax.broadcasted_iota(jnp.int32, rows.shape, 1) < HD
    zero = jnp.zeros_like(rows)
    return jnp.concatenate([jnp.where(first, rows, zero), jnp.where(first, zero, rows)], 0)


def own_lanes(rows):
    half = rows.shape[0] // 2
    first = lax.broadcasted_iota(jnp.int32, (half, rows.shape[1]), 1) < HD
    return jnp.where(first, rows[:half], rows[half:])


def attend_kernel(
    uq, uk, uv, kq, kk, kv, same_one, same_two, key_ids, query_ids, out, probs, cq, ck, cv, bias
):
    tiles = query_ids.shape[1] // TILE

    @pl.when(pl.program_id(0) == 0)
    def _():
        for t in range(tiles):
            rows = lax.broadcasted_iota(jnp.int32, (WINDOW, TILE), 0)
            columns = lax.broadcasted_iota(jnp.int32, (WINDOW, TILE), 1) + REACH
            equal = key_ids[t * TILE : t * TILE + WINDOW] == query_ids[:, t * TILE : (t + 1) * TILE]
            allowed = (equal & (rows <= columns)) | (rows == columns)
            tile_bias = jnp.where(allowed, 0.0, MASKED)
            bias[t] = jnp.concatenate([tile_bias, tile_bias], 1)

    one, two = same_one[...], same_two[...]

    def convolved(u, taps):
        field = u[...].astype(jnp.float32)
        return (
            taps[0:1] * field
            + taps[1:2] * pltpu.roll(field, 1, 0) * one
            + taps[2:3] * pltpu.roll(field, 2, 0) * two
        )

    cq[...] = convolved(uq, kq)[REACH:].astype(jnp.bfloat16) * 0.125
    ck[...] = convolved(uk, kk).astype(jnp.bfloat16)
    cv[...] = convolved(uv, kv).astype(jnp.bfloat16)
    for t in range(tiles):
        window = slice(t * TILE, t * TILE + WINDOW)
        own = slice(t * TILE, (t + 1) * TILE)
        scores = dot(ck[window], both_heads(cq[own]), 1, 1) + bias[t]
        powers = jnp.exp(scores - jnp.max(scores, 0, keepdims=True))
        narrow = (powers * (1.0 / jnp.sum(powers, 0, keepdims=True))).astype(jnp.bfloat16)
        probs[0, t] = narrow
        out[own] = own_lanes(dot(narrow, cv[window], 0, 0)).astype(jnp.bfloat16)


def attend_back_kernel(
    grad_out, probs, cq, ck, cv, uq, uk, uv, kq, kk, kv, same_one, same_two,
    gu, gtaps, gq_rows, gk_rows, gv_rows,
):
    head = pl.program_id(0)
    width = gu.shape[1] // 3
    tiles = grad_out.shape[0] // TILE
    gq_rows[:REACH] = jnp.zeros((REACH, PAIR), jnp.float32)
    gk_rows[...] = jnp.zeros_like(gk_rows)
    gv_rows[...] = jnp.zeros_like(gv_rows)
    for t in range(tiles):
        window = slice(t * TILE, t * TILE + WINDOW)
        own = slice(t * TILE, (t + 1) * TILE)
        grads = both_heads(grad_out[own])
        narrow = probs[0, t]
        wide = narrow.astype(jnp.float32)
        grad_probs = dot(cv[window], grads, 1, 1)
        delta = jnp.sum(wide * grad_probs, 0, keepdims=True)
        grad_scores = (wide * (grad_probs - delta)).astype(jnp.bfloat16)
        gk_rows[window] += dot(grad_scores, both_heads(cq[own]), 1, 0)
        gv_rows[window] += dot(narrow, grads, 1, 0)
        gq_rows[REACH + t * TILE : REACH + (t + 1) * TILE] = (
            own_lanes(dot(grad_scores, ck[window], 0, 0)) * 0.125
        )
    one, two = same_one[...], same_two[...]
    last = gq_rows.shape[0]
    for part, (rows, u, taps) in enumerate(
        ((gq_rows, uq, kq), (gk_rows, uk, kk), (gv_rows, uv, kv))
    ):
        field = u[...].astype(jnp.float32)
        grad = rows[...]
        grad_one, grad_two = grad * one, grad * two
        place = pl.ds(pl.multiple_of(part * width + head * PAIR, PAIR), PAIR)
        gu[:, place] = (
            taps[0:1] * grad
            + taps[1:2] * pltpu.roll(grad_one, last - 1, 0)
            + taps[2:3] * pltpu.roll(grad_two, last - 2, 0)
        ).astype(jnp.bfloat16)
        gtaps[0:1, place] = jnp.sum(grad * field, 0, keepdims=True)
        gtaps[1:2, place] = jnp.sum(grad_one * pltpu.roll(field, 1, 0), 0, keepdims=True)
        gtaps[2:3, place] = jnp.sum(grad_two * pltpu.roll(field, 2, 0), 0, keepdims=True)


def column_specs(rows, pairs):
    return [
        pl.BlockSpec((rows, PAIR), lambda h, part=part: (0, part * pairs + h)) for part in range(3)
    ]


def whole(shape):
    return pl.BlockSpec(shape, lambda h: (0,) * len(shape))


def attend(mixed, taps, same_one, same_two, key_ids, query_ids):
    rows, width = mixed.shape[0], mixed.shape[1] // 3
    slots, pairs = rows - REACH, width // PAIR
    tiles = slots // TILE
    block = lambda count: pl.BlockSpec((count, PAIR), lambda h: (0, h))
    return pl.pallas_call(
        attend_kernel,
        grid=(pairs,),
        in_specs=column_specs(rows, pairs)
        + column_specs(3, pairs)
        + [whole((rows, 1))] * 3
        + [whole((1, slots))],
        out_specs=[
            block(slots),
            pl.BlockSpec((1, tiles, WINDOW, 2 * TILE), lambda h: (h, 0, 0, 0)),
            block(slots),
            block(rows),
            block(rows),
        ],
        out_shape=[
            jax.ShapeDtypeStruct((slots, width), jnp.bfloat16),
            jax.ShapeDtypeStruct((pairs, tiles, WINDOW, 2 * TILE), jnp.bfloat16),
            jax.ShapeDtypeStruct((slots, width), jnp.bfloat16),
            jax.ShapeDtypeStruct((rows, width), jnp.bfloat16),
            jax.ShapeDtypeStruct((rows, width), jnp.bfloat16),
        ],
        scratch_shapes=[pltpu.VMEM((tiles, WINDOW, 2 * TILE), jnp.float32)],
        name="attend",
    )(mixed, mixed, mixed, taps, taps, taps, same_one, same_two, key_ids, query_ids)


def attend_back(grad_heads, kept, mixed, taps, same_one, same_two):
    rows, width = mixed.shape[0], mixed.shape[1] // 3
    slots, pairs = rows - REACH, width // PAIR
    tiles = slots // TILE
    probs, cq, ck, cv = kept
    block = lambda count: pl.BlockSpec((count, PAIR), lambda h: (0, h))
    return pl.pallas_call(
        attend_back_kernel,
        grid=(pairs,),
        in_specs=[
            block(slots),
            pl.BlockSpec((1, tiles, WINDOW, 2 * TILE), lambda h: (h, 0, 0, 0)),
            block(slots),
            block(rows),
            block(rows),
        ]
        + column_specs(rows, pairs)
        + column_specs(3, pairs)
        + [whole((rows, 1))] * 2,
        out_specs=[whole((rows, 3 * width)), whole((3, 3 * width))],
        out_shape=[
            jax.ShapeDtypeStruct((rows, 3 * width), jnp.bfloat16),
            jax.ShapeDtypeStruct((3, 3 * width), jnp.float32),
        ],
        scratch_shapes=[pltpu.VMEM((rows, PAIR), jnp.float32)] * 3,
        name="attend_back",
    )(grad_heads, probs, cq, ck, cv, mixed, mixed, mixed, taps, taps, taps, same_one, same_two)


def partner(block, axis, bit):
    return lax.ppermute(block, axis, [(i, i ^ bit) for i in range(lax.axis_size(axis))])


def bits_of(axis):
    return [(axis, 1 << k) for k in range(lax.axis_size(axis).bit_length() - 1)]


def upper(axis, bit):
    return (lax.axis_index(axis) // bit) % 2


def exchange_orders():
    core, *along_y = bits_of("stream")
    along_seq = bits_of("seq")
    along_x, along_z = along_seq[: len(along_y)], along_seq[len(along_y) :]
    near, far = along_z[:1], along_z[1:]
    return core, (along_y + along_x + near + far, along_x + near + along_y + far, near + along_y + along_x + far)


def halved(block, axis, bit):
    half = block.shape[0] // 2
    at = upper(axis, bit)
    keep = lax.dynamic_slice_in_dim(block, at * half, half)
    send = lax.dynamic_slice_in_dim(block, (1 - at) * half, half)
    return (keep.astype(jnp.float32) + partner(send, axis, bit).astype(jnp.float32)).astype(block.dtype)


def doubled(block, axis, bit):
    other = partner(block, axis, bit)
    return jnp.where(
        upper(axis, bit) == 0,
        jnp.concatenate([block, other]),
        jnp.concatenate([other, block]),
    )


def scattered(bucket):
    core, orders = exchange_orders()
    mine = halved(bucket, *core)
    third = mine.shape[0] // 3
    chunks = [mine[k * third : (k + 1) * third] for k in range(3)]
    steps = len(orders[0])
    for step in range(steps):
        chunks = [halved(chunk, *order[step]) for chunk, order in zip(chunks, orders)]
    return chunks


def gathered(chunks):
    core, orders = exchange_orders()
    for step in reversed(range(len(orders[0]))):
        chunks = [doubled(chunk, *order[step]) for chunk, order in zip(chunks, orders)]
    others = [partner(chunk, *core) for chunk in chunks]
    lower = upper(*core) == 0
    return jnp.where(
        lower, jnp.concatenate(chunks + others), jnp.concatenate(others + chunks)
    ).astype(jnp.float32)


def summed_small(pieces):
    total = jnp.concatenate([piece.reshape(-1, 128) for piece in pieces])
    for axis, bit in bits_of("stream") + bits_of("seq"):
        total = total + partner(total, axis, bit)
    parts, offset = [], 0
    for piece in pieces:
        count = piece.size // 128
        parts.append(total[offset : offset + count].reshape(piece.shape))
        offset += count
    return parts


def wide_of(blocks, width):
    return jnp.concatenate([blocks[k : k + width] for k in range(0, blocks.shape[0], width)], 1)


def passed_along(block, axis, distance):
    devices = range(lax.axis_size(axis))
    route = [(i - distance, i) for i in devices if i - distance in devices]
    return lax.ppermute(block, axis, route)


def product(left, right, left_dim, right_dim, dtype=jnp.float32):
    return dot(left, right, left_dim, right_dim).astype(dtype)


def on_device(
    tokens,
    segment_ids,
    query_key_value_weight,
    conv_kernel,
    attention_output_weight,
    up_weight,
    down_weight,
    gain_attn,
    shift_attn,
    gain_ffn,
    shift_ffn,
    cotangent,
):
    narrow = jnp.bfloat16
    own_tokens, ids, grad_low = tokens[0], segment_ids[0], cotangent[0]
    prior_tokens, prior_ids = passed_along((own_tokens[-REACH:], ids[-REACH:]), "seq", 1)
    prior_ids = jnp.where(lax.axis_index("seq") > 0, prior_ids, -1)
    rows_ids = jnp.concatenate([prior_ids, ids])
    live_rows = rows_ids >= 0

    def same(distance):
        moved = jnp.concatenate([jnp.full((distance,), -1, jnp.int32), rows_ids[:-distance]])
        return ((moved == rows_ids) & live_rows).astype(jnp.float32)[:, None]

    same_one, same_two = same(1), same(2)
    key_ids = jnp.where(live_rows, rows_ids, -2)[:, None]
    live = (ids >= 0).astype(jnp.float32)[:, None]
    taps = conv_kernel.astype(jnp.float32)

    rows = jnp.concatenate([prior_tokens, own_tokens]).astype(jnp.float32)
    first, first_back = jax.vjp(
        layer_norm, rows, gain_attn.astype(jnp.float32), shift_attn.astype(jnp.float32)
    )
    first = first.astype(narrow)
    mixed = product(first, query_key_value_weight, 1, 0, narrow)
    attended, *kept = attend(mixed, taps, same_one, same_two, key_ids, ids[None])

    middle = own_tokens.astype(jnp.float32) + live * product(attended, attention_output_weight, 1, 0)
    second, second_back = jax.vjp(
        layer_norm, middle, gain_ffn.astype(jnp.float32), shift_ffn.astype(jnp.float32)
    )
    second = second.astype(narrow)
    hidden = jnp.maximum(product(second, up_weight, 1, 0), 0.0)
    active = jnp.square(hidden).astype(narrow)
    grad = grad_low.astype(jnp.float32)
    grad_branch = (live * grad).astype(narrow)
    grad_w_down = product(active, grad_branch, 0, 0, narrow)
    grad_hidden = (product(grad_branch, down_weight, 1, 1) * (2.0 * hidden)).astype(narrow)
    width = second.shape[1]
    grad_w_up = [
        product(second, grad_hidden[:, k : k + width], 0, 0, narrow)
        for k in range(0, grad_hidden.shape[1], width)
    ]
    forward_chunks = scattered(jnp.concatenate([grad_w_down] + grad_w_up))
    out_tokens = (middle + live * product(active, down_weight, 1, 0)).astype(narrow)
    grad_part, grad_gain_ffn, grad_shift_ffn = second_back(product(grad_hidden, up_weight, 1, 1))
    grad_middle = grad + grad_part
    grad_attended = (live * grad_middle).astype(narrow)
    grad_w_out = product(attended, grad_attended, 0, 0, narrow)
    grad_heads = product(grad_attended, attention_output_weight, 1, 1, narrow)

    grad_mixed, grad_taps = attend_back(grad_heads, kept, mixed, taps, same_one, same_two)
    grad_w_qkv = [
        product(first, grad_mixed[:, k : k + width], 0, 0, narrow)
        for k in range(0, grad_mixed.shape[1], width)
    ]
    attention_chunks = scattered(jnp.concatenate([grad_w_out] + grad_w_qkv))
    grad_rows, grad_gain_attn, grad_shift_attn = first_back(
        product(grad_mixed, query_key_value_weight, 1, 1)
    )
    later = passed_along(grad_rows[:REACH].astype(narrow), "seq", -1)
    grad_tokens = grad_middle + grad_rows[REACH:]
    slots = grad_tokens.shape[0]
    grad_tokens = grad_tokens + jnp.pad(
        later.astype(jnp.float32), ((slots - REACH, 0), (0, 0))
    )
    forward_sum = gathered(forward_chunks)
    attention_sum = gathered(attention_chunks)
    parts = summed_small(
        [grad_taps, grad_gain_attn, grad_shift_attn, grad_gain_ffn, grad_shift_ffn]
    )
    units = grad_w_down.shape[0]
    return (
        out_tokens[None],
        grad_tokens[None],
        wide_of(attention_sum[width:], width),
        parts[0],
        attention_sum[:width],
        wide_of(forward_sum[units:], width),
        forward_sum[:units],
        parts[1],
        parts[2],
        parts[3],
        parts[4],
    )


def solution(mesh):
    return jax.shard_map(
        on_device,
        mesh=mesh,
        in_specs=(
            P("stream", "seq", None),
            P("stream", "seq"),
            P(),
            P(),
            P(),
            P(),
            P(),
            P(),
            P(),
            P(),
            P(),
            P("stream", "seq", None),
        ),
        out_specs=(
            P("stream", "seq", None),
            P("stream", "seq", None),
            P(),
            P(),
            P(),
            P(),
            P(),
            P(),
            P(),
            P(),
            P(),
        ),
        check_vma=False,
    )
```

```python
import jax
import jax.numpy as jnp
from jax import lax
from jax.experimental import pallas as pl
from jax.experimental.pallas import tpu as pltpu
from jax.sharding import PartitionSpec as P


HD = 64
PAIR = 2 * HD
EPSILON = 1e-05
MASKED = -1e30
REACH = 256
TILE = 128
WINDOW = REACH + TILE


def layer_norm(field, gain, shift):
    center = field - jnp.mean(field, -1, keepdims=True)
    spread = jnp.mean(center * center, -1, keepdims=True)
    return center * lax.rsqrt(spread + EPSILON) * gain + shift


def dot(left, right, left_dim, right_dim):
    return lax.dot_general(
        left, right, (((left_dim,), (right_dim,)), ((), ())), preferred_element_type=jnp.float32
    )


def both_heads(rows):
    first = lax.broadcasted_iota(jnp.int32, rows.shape, 1) < HD
    zero = jnp.zeros_like(rows)
    return jnp.concatenate([jnp.where(first, rows, zero), jnp.where(first, zero, rows)], 0)


def own_lanes(rows):
    half = rows.shape[0] // 2
    first = lax.broadcasted_iota(jnp.int32, (half, rows.shape[1]), 1) < HD
    return jnp.where(first, rows[:half], rows[half:])


def attend_kernel(
    uq, uk, uv, kq, kk, kv, same_one, same_two, key_ids, query_ids, out, probs, cq, ck, cv, bias
):
    tiles = query_ids.shape[1] // TILE

    @pl.when(pl.program_id(0) == 0)
    def _():
        for t in range(tiles):
            rows = lax.broadcasted_iota(jnp.int32, (WINDOW, TILE), 0)
            columns = lax.broadcasted_iota(jnp.int32, (WINDOW, TILE), 1) + REACH
            equal = key_ids[t * TILE : t * TILE + WINDOW] == query_ids[:, t * TILE : (t + 1) * TILE]
            allowed = (equal & (rows <= columns)) | (rows == columns)
            tile_bias = jnp.where(allowed, 0.0, MASKED)
            bias[t] = jnp.concatenate([tile_bias, tile_bias], 1)

    one, two = same_one[...], same_two[...]

    def convolved(u, taps):
        field = u[...].astype(jnp.float32)
        taps = taps[...].astype(jnp.float32)
        return (
            taps[0:1] * field
            + taps[1:2] * pltpu.roll(field, 1, 0) * one
            + taps[2:3] * pltpu.roll(field, 2, 0) * two
        )

    cq[...] = convolved(uq, kq)[REACH:].astype(jnp.bfloat16) * 0.125
    ck[...] = convolved(uk, kk).astype(jnp.bfloat16)
    cv[...] = convolved(uv, kv).astype(jnp.bfloat16)
    for t in range(tiles):
        window = slice(t * TILE, t * TILE + WINDOW)
        own = slice(t * TILE, (t + 1) * TILE)
        scores = dot(ck[window], both_heads(cq[own]), 1, 1) + bias[t]
        powers = jnp.exp(scores - jnp.max(scores, 0, keepdims=True))
        narrow = (powers * (1.0 / jnp.sum(powers, 0, keepdims=True))).astype(jnp.bfloat16)
        probs[0, t] = narrow
        out[own] = own_lanes(dot(narrow, cv[window], 0, 0)).astype(jnp.bfloat16)


def attend_back_kernel(
    grad_out, probs, cq, ck, cv, uq, uk, uv, kq, kk, kv, same_one, same_two,
    gu, gtaps, gq_rows, gk_rows, gv_rows,
):
    head = pl.program_id(0)
    width = gu.shape[1] // 3
    tiles = grad_out.shape[0] // TILE
    gq_rows[:REACH] = jnp.zeros((REACH, PAIR), jnp.float32)
    gk_rows[...] = jnp.zeros_like(gk_rows)
    gv_rows[...] = jnp.zeros_like(gv_rows)
    for t in range(tiles):
        window = slice(t * TILE, t * TILE + WINDOW)
        own = slice(t * TILE, (t + 1) * TILE)
        grads = both_heads(grad_out[own])
        narrow = probs[0, t]
        wide = narrow.astype(jnp.float32)
        grad_probs = dot(cv[window], grads, 1, 1)
        delta = jnp.sum(wide * grad_probs, 0, keepdims=True)
        grad_scores = (wide * (grad_probs - delta)).astype(jnp.bfloat16)
        gk_rows[window] += dot(grad_scores, both_heads(cq[own]), 1, 0)
        gv_rows[window] += dot(narrow, grads, 1, 0)
        gq_rows[REACH + t * TILE : REACH + (t + 1) * TILE] = (
            own_lanes(dot(grad_scores, ck[window], 0, 0)) * 0.125
        )
    one, two = same_one[...], same_two[...]
    last = gq_rows.shape[0]
    for part, (rows, u, taps) in enumerate(
        ((gq_rows, uq, kq), (gk_rows, uk, kk), (gv_rows, uv, kv))
    ):
        field = u[...].astype(jnp.float32)
        grad = rows[...]
        taps = taps[...].astype(jnp.float32)
        grad_one, grad_two = grad * one, grad * two
        place = pl.ds(pl.multiple_of(part * width + head * PAIR, PAIR), PAIR)
        gu[:, place] = (
            taps[0:1] * grad
            + taps[1:2] * pltpu.roll(grad_one, last - 1, 0)
            + taps[2:3] * pltpu.roll(grad_two, last - 2, 0)
        ).astype(jnp.bfloat16)
        lanes = pl.ds(pl.multiple_of(head * PAIR, PAIR), PAIR)
        for lag, lagged in enumerate(
            (
                grad * field,
                grad_one * pltpu.roll(field, 1, 0),
                grad_two * pltpu.roll(field, 2, 0),
            )
        ):
            gtaps[3 * lag + part : 3 * lag + part + 1, lanes] = jnp.sum(lagged, 0, keepdims=True)


def column_specs(rows, pairs):
    return [
        pl.BlockSpec((rows, PAIR), lambda h, part=part: (0, part * pairs + h)) for part in range(3)
    ]


def whole(shape):
    return pl.BlockSpec(shape, lambda h: (0,) * len(shape))


def attend(mixed, taps, same_one, same_two, key_ids, query_ids):
    rows, width = mixed.shape[0], mixed.shape[1] // 3
    slots, pairs = rows - REACH, width // PAIR
    tiles = slots // TILE
    block = lambda count: pl.BlockSpec((count, PAIR), lambda h: (0, h))
    return pl.pallas_call(
        attend_kernel,
        grid=(pairs,),
        in_specs=column_specs(rows, pairs)
        + column_specs(3, pairs)
        + [whole((rows, 1))] * 3
        + [whole((1, slots))],
        out_specs=[
            block(slots),
            pl.BlockSpec((1, tiles, WINDOW, 2 * TILE), lambda h: (h, 0, 0, 0)),
            block(slots),
            block(rows),
            block(rows),
        ],
        out_shape=[
            jax.ShapeDtypeStruct((slots, width), jnp.bfloat16),
            jax.ShapeDtypeStruct((pairs, tiles, WINDOW, 2 * TILE), jnp.bfloat16),
            jax.ShapeDtypeStruct((slots, width), jnp.bfloat16),
            jax.ShapeDtypeStruct((rows, width), jnp.bfloat16),
            jax.ShapeDtypeStruct((rows, width), jnp.bfloat16),
        ],
        scratch_shapes=[pltpu.VMEM((tiles, WINDOW, 2 * TILE), jnp.float32)],
        name="attend",
    )(mixed, mixed, mixed, taps, taps, taps, same_one, same_two, key_ids, query_ids)


def attend_back(grad_heads, kept, mixed, taps, same_one, same_two):
    rows, width = mixed.shape[0], mixed.shape[1] // 3
    slots, pairs = rows - REACH, width // PAIR
    tiles = slots // TILE
    probs, cq, ck, cv = kept
    block = lambda count: pl.BlockSpec((count, PAIR), lambda h: (0, h))
    return pl.pallas_call(
        attend_back_kernel,
        grid=(pairs,),
        in_specs=[
            block(slots),
            pl.BlockSpec((1, tiles, WINDOW, 2 * TILE), lambda h: (h, 0, 0, 0)),
            block(slots),
            block(rows),
            block(rows),
        ]
        + column_specs(rows, pairs)
        + column_specs(3, pairs)
        + [whole((rows, 1))] * 2,
        out_specs=[whole((rows, 3 * width)), whole((9, width))],
        out_shape=[
            jax.ShapeDtypeStruct((rows, 3 * width), jnp.bfloat16),
            jax.ShapeDtypeStruct((9, width), jnp.float32),
        ],
        scratch_shapes=[pltpu.VMEM((rows, PAIR), jnp.float32)] * 3,
        name="attend_back",
    )(grad_heads, probs, cq, ck, cv, mixed, mixed, mixed, taps, taps, taps, same_one, same_two)


def project_kernel(prior, own, gain, shift, weight, first, mixed):
    @pl.when(pl.program_id(0) == 0)
    def _():
        rows = jnp.concatenate([prior[...], own[...]]).astype(jnp.float32)
        scale, offset = gain[...].astype(jnp.float32), shift[...].astype(jnp.float32)
        first[...] = layer_norm(rows, scale, offset).astype(jnp.bfloat16)

    mixed[...] = dot(first[...], weight[...], 1, 0).astype(jnp.bfloat16)


def project(prior, own, gain, shift, weight):
    width = own.shape[1]
    rows, part = prior.shape[0] + own.shape[0], width // 2
    return pl.pallas_call(
        project_kernel,
        grid=(weight.shape[1] // part,),
        in_specs=[whole(prior.shape), whole(own.shape)]
        + [whole((1, width))] * 2
        + [pl.BlockSpec((width, part), lambda s: (0, s))],
        out_specs=[whole((rows, width)), pl.BlockSpec((rows, part), lambda s: (0, s))],
        out_shape=[
            jax.ShapeDtypeStruct((rows, width), jnp.bfloat16),
            jax.ShapeDtypeStruct((rows, weight.shape[1]), jnp.bfloat16),
        ],
        name="project",
    )(prior, own, gain[None], shift[None], weight)


def bucket_kernel(attended, grad_attended, first, grad_mixed, grads):
    step = pl.program_id(0)

    @pl.when(step == 0)
    def _():
        grads[...] = dot(attended[...], grad_attended[...], 0, 0).astype(jnp.bfloat16)

    @pl.when(step > 0)
    def _():
        grads[...] = dot(first[...], grad_mixed[...], 0, 0).astype(jnp.bfloat16)


def attention_bucket(attended, grad_attended, first, grad_mixed):
    slots, width = attended.shape
    rows = first.shape[0]
    return pl.pallas_call(
        bucket_kernel,
        grid=(4,),
        in_specs=[whole((slots, width)), whole((slots, width)), whole((rows, width))]
        + [pl.BlockSpec((rows, width), lambda s: (0, jnp.maximum(s - 1, 0)))],
        out_specs=pl.BlockSpec((width, width), lambda s: (s, 0)),
        out_shape=jax.ShapeDtypeStruct((4 * width, width), jnp.bfloat16),
        name="attention_bucket",
    )(attended, grad_attended, first, grad_mixed)


def feed_kernel(second, grad_branch, up, down, grads, out, grad_second):
    @pl.when(pl.program_id(0) == 0)
    def _():
        out[...] = jnp.zeros_like(out)
        grad_second[...] = jnp.zeros_like(grad_second)

    hidden = jnp.maximum(dot(second[...], up[...], 1, 0), 0.0)
    active = jnp.square(hidden).astype(jnp.bfloat16)
    grads[0, 0] = dot(active, grad_branch[...], 0, 0).astype(jnp.bfloat16)
    grad_hidden = (dot(grad_branch[...], down[...], 1, 1) * (2.0 * hidden)).astype(jnp.bfloat16)
    grads[1, 0] = dot(second[...], grad_hidden, 0, 0).astype(jnp.bfloat16)
    grad_second[...] += dot(grad_hidden, up[...], 1, 1)
    out[...] += dot(active, down[...], 1, 0)


def feed(second, grad_branch, up_weight, down_weight):
    slots, width = second.shape
    steps = up_weight.shape[1] // width
    return pl.pallas_call(
        feed_kernel,
        grid=(steps,),
        in_specs=[
            whole((slots, width)),
            whole((slots, width)),
            pl.BlockSpec((width, width), lambda f: (0, f)),
            pl.BlockSpec((width, width), lambda f: (f, 0)),
        ],
        out_specs=[
            pl.BlockSpec((2, 1, width, width), lambda f: (0, f, 0, 0)),
            whole((slots, width)),
            whole((slots, width)),
        ],
        out_shape=[
            jax.ShapeDtypeStruct((2, steps, width, width), jnp.bfloat16),
            jax.ShapeDtypeStruct((slots, width), jnp.float32),
            jax.ShapeDtypeStruct((slots, width), jnp.float32),
        ],
        name="feed",
    )(second, grad_branch, up_weight, down_weight)


def partner(block, axis, bit):
    return lax.ppermute(block, axis, [(i, i ^ bit) for i in range(lax.axis_size(axis))])


def bits_of(axis):
    return [(axis, 1 << k) for k in range(lax.axis_size(axis).bit_length() - 1)]


def upper(axis, bit):
    return (lax.axis_index(axis) // bit) % 2


def exchange_orders():
    core, *along_y = bits_of("stream")
    along_seq = bits_of("seq")
    along_x, along_z = along_seq[: len(along_y)], along_seq[len(along_y) :]
    near, far = along_z[:1], along_z[1:]
    return core, (
        along_y + along_x + near + far,
        along_x + near + along_y + far,
        near + along_y + along_x + far,
    )


def halved(block, left, step):
    at, place = upper(*step), left.index(step)
    keep = lax.dynamic_index_in_dim(block, at, place, keepdims=False)
    send = lax.dynamic_index_in_dim(block, 1 - at, place, keepdims=False)
    other = partner(send, *step)
    total = keep.astype(jnp.float32) + other.astype(jnp.float32)
    return total.astype(block.dtype), [bit for bit in left if bit != step]


def scattered(bucket):
    core, orders = exchange_orders()
    left = bits_of("seq")[::-1] + bits_of("stream")[::-1]
    rows = bucket.shape[0] // (3 << len(left))
    blocks = bucket.reshape((2,) * len(left) + (3 * rows, -1))
    mine, left = halved(blocks, left, core)
    chunks = [
        (lax.slice_in_dim(mine, k * rows, (k + 1) * rows, axis=len(left)), left) for k in range(3)
    ]
    for step in range(len(left)):
        chunks = [halved(*chunk, order[step]) for chunk, order in zip(chunks, orders)]
    return [chunk for chunk, _ in chunks]


def gathered(chunks):
    core, orders = exchange_orders()
    every = bits_of("seq")[::-1] + bits_of("stream")[:0:-1]
    have = [[] for _ in chunks]
    for step in reversed(range(len(every))):
        for k, order in enumerate(orders):
            bit = order[step]
            have[k] = [other for other in every if other in have[k] + [bit]]
            place = have[k].index(bit)
            other = partner(chunks[k], *bit)
            chunks[k] = jnp.where(
                upper(*bit) == 0,
                jnp.stack([chunks[k], other], place),
                jnp.stack([other, chunks[k]], place),
            )
    flat = [chunk.reshape((-1,) + chunk.shape[-2:]) for chunk in chunks]
    others = []
    for chunk in flat:
        others.append(partner(chunk, *core))
    return flat, others


def summed_small(pieces):
    total = jnp.concatenate(pieces)
    for bit in bits_of("stream") + bits_of("seq"):
        other = partner(total, *bit)
        total = total + other
    return total


def laid_out(halves, width, first_blocks, blocks):
    own, other = halves
    piece = own[0].shape[1]
    rows = 12 * piece
    per = width // rows
    first_steps = first_blocks * per
    beside = blocks - first_blocks

    def side(s):
        at = jnp.maximum(s - first_steps, 0)
        return (at % per, at // per)

    return pl.pallas_call(
        lambda *refs: paired_kernel(first_steps, *refs),
        grid=(blocks * per,),
        in_specs=[pl.BlockSpec(memory_space=pltpu.SMEM)]
        + [pl.BlockSpec((2, piece, width), lambda s: (s, 0, 0))] * 6,
        out_specs=[
            pl.BlockSpec((rows, width), lambda s: (jnp.minimum(s, first_steps - 1), 0)),
            pl.BlockSpec((rows, width), side),
        ],
        out_shape=[
            jax.ShapeDtypeStruct((first_blocks * width, width), jnp.float32),
            jax.ShapeDtypeStruct((width, beside * width), jnp.float32),
        ],
    )(upper(*exchange_orders()[0]).reshape(1), *own, *other)


def stored(first_steps, first, second, value):
    step = pl.program_id(0)

    @pl.when(step < first_steps)
    def _():
        first[...] = value

    @pl.when(step >= first_steps)
    def _():
        second[...] = value


def paired_kernel(first_steps, side, a, b, c, d, e, f, first, second):
    lower = side[0] == 0
    parts = []
    for at in range(a.shape[0]):
        own = jnp.concatenate([ref[at].astype(jnp.float32) for ref in (a, b, c)])
        other = jnp.concatenate([ref[at].astype(jnp.float32) for ref in (d, e, f)])
        parts += [jnp.where(lower, own, other), jnp.where(lower, other, own)]
    stored(first_steps, first, second, jnp.concatenate(parts))


def passed_along(block, axis, distance):
    devices = range(lax.axis_size(axis))
    route = [(i - distance, i) for i in devices if i - distance in devices]
    return lax.ppermute(block, axis, route)


def product(left, right, left_dim, right_dim, dtype=jnp.float32):
    return dot(left, right, left_dim, right_dim).astype(dtype)


def on_device(
    tokens,
    segment_ids,
    query_key_value_weight,
    conv_kernel,
    attention_output_weight,
    up_weight,
    down_weight,
    gain_attn,
    shift_attn,
    gain_ffn,
    shift_ffn,
    cotangent,
):
    narrow = jnp.bfloat16
    own_tokens, ids, grad_low = tokens[0], segment_ids[0], cotangent[0]
    prior_tokens, prior_ids = passed_along((own_tokens[-REACH:], ids[-REACH:]), "seq", 1)
    prior_ids = jnp.where(lax.axis_index("seq") > 0, prior_ids, -1)
    rows_ids = jnp.concatenate([prior_ids, ids])
    live_rows = rows_ids >= 0

    def same(distance):
        moved = jnp.concatenate([jnp.full((distance,), -1, jnp.int32), rows_ids[:-distance]])
        return ((moved == rows_ids) & live_rows).astype(jnp.float32)[:, None]

    same_one, same_two = same(1), same(2)
    key_ids = jnp.where(live_rows, rows_ids, -2)[:, None]
    live = (ids >= 0).astype(jnp.float32)[:, None]
    taps = conv_kernel

    rows = jnp.concatenate([prior_tokens, own_tokens]).astype(jnp.float32)
    _, first_back = jax.vjp(
        layer_norm, rows, gain_attn.astype(jnp.float32), shift_attn.astype(jnp.float32)
    )
    first, mixed = project(
        prior_tokens, own_tokens, gain_attn, shift_attn, query_key_value_weight
    )
    attended, *kept = attend(mixed, taps, same_one, same_two, key_ids, ids[None])

    middle = own_tokens.astype(jnp.float32) + live * product(attended, attention_output_weight, 1, 0)
    second, second_back = jax.vjp(
        layer_norm, middle, gain_ffn.astype(jnp.float32), shift_ffn.astype(jnp.float32)
    )
    second = second.astype(narrow)
    grad = grad_low.astype(jnp.float32)
    grad_branch = (live * grad).astype(narrow)
    feed_grads, feed_out, grad_second = feed(second, grad_branch, up_weight, down_weight)
    width = second.shape[1]
    out_tokens = (middle + live * feed_out).astype(narrow)
    feed_chunks = scattered(feed_grads.reshape(-1, width))
    grad_part, grad_gain_ffn, grad_shift_ffn = second_back(grad_second)
    grad_middle = grad + grad_part
    grad_attended = (live * grad_middle).astype(narrow)
    grad_heads = product(grad_attended, attention_output_weight, 1, 1, narrow)

    grad_mixed, grad_taps = attend_back(grad_heads, kept, mixed, taps, same_one, same_two)
    attention_grads = attention_bucket(attended, grad_attended, first, grad_mixed)
    attention_chunks = scattered(attention_grads)
    grad_first = product(grad_mixed, query_key_value_weight, 1, 1)
    grad_rows, grad_gain_attn, grad_shift_attn = first_back(grad_first)
    later = passed_along(grad_rows[:REACH].astype(narrow), "seq", -1)
    grad_tokens = grad_middle + grad_rows[REACH:]
    slots = grad_tokens.shape[0]
    grad_tokens = grad_tokens + jnp.pad(
        later.astype(jnp.float32), ((slots - REACH, 0), (0, 0))
    )
    feed_halves = gathered(feed_chunks)
    attention_halves = gathered(attention_chunks)
    rows_sum = summed_small(
        [grad_taps]
        + [row[None] for row in (grad_gain_attn, grad_shift_attn, grad_gain_ffn, grad_shift_ffn)]
    )
    parts = [rows_sum[:9].reshape(conv_kernel.shape)] + [rows_sum[k] for k in range(9, 13)]
    feed_blocks = up_weight.shape[1] // width
    grad_w_down, grad_w_up = laid_out(feed_halves, width, feed_blocks, 2 * feed_blocks)
    grad_w_out, grad_w_qkv = laid_out(attention_halves, width, 1, 4)
    return (
        out_tokens[None],
        grad_tokens[None],
        grad_w_qkv,
        parts[0],
        grad_w_out,
        grad_w_up,
        grad_w_down,
        parts[1],
        parts[2],
        parts[3],
        parts[4],
    )


def solution(mesh):
    return jax.shard_map(
        on_device,
        mesh=mesh,
        in_specs=(
            P("stream", "seq", None),
            P("stream", "seq"),
            P(),
            P(),
            P(),
            P(),
            P(),
            P(),
            P(),
            P(),
            P(),
            P("stream", "seq", None),
        ),
        out_specs=(
            P("stream", "seq", None),
            P("stream", "seq", None),
            P(),
            P(),
            P(),
            P(),
            P(),
            P(),
            P(),
            P(),
            P(),
        ),
        check_vma=False,
    )
```
